32 devices in a mesh: ep: 32 (over z, y, x, core), kv: 1.
Axes of the slice: x: 2, y: 2, z: 4, core: 2. Of those that a mesh axis runs over, the one named last changes fastest.
Arguments:
- tokens: bfloat16 [4096, 2560], P('ep'), may hold values from -6 to 6
- routes: int32 [4096, 6], P('ep'), may hold values from 0 to 15, all different within a row; in each aligned block of 128 rows (0 to 127, 128 to 255, ...) at most 64 rows name the same one
- route_weights: float32 [4096, 6], P('ep'), may hold values from 0.05 to 0.4
- w_gate: bfloat16 [32, 2560, 768], P('ep', None, 'kv'), may hold values from -0.125 to 0.125
- w_up: bfloat16 [32, 2560, 768], P('ep', None, 'kv'), may hold values from -0.125 to 0.125
- w_down: bfloat16 [32, 768, 2560], P('ep', 'kv'), may hold values from -0.15625 to 0.15625
- queries: bfloat16 [32, 2560], P('ep')
- key_cache: bfloat16 [32, 1024, 512], P('ep', 'kv')
- value_cache: bfloat16 [32, 1024, 512], P('ep', 'kv'), may hold values from -6 to 6
- lengths: int32 [32], P('ep'), may hold values from 1 to 1024, as said below
Outputs:
- moe_out: bfloat16 [4096, 2560], P('ep')
- attn_out: bfloat16 [32, 2560], P('ep')
The draws below stay inside these ranges and needn't reach their ends.
Inputs may be any that keep to these rules, and one draw needn't show every extreme that they name: `routes`: each row names 6 different experts; among the rows of one index of ep no expert is named by more than 64 rows, a bound that some block reaches of them. Request r uses cache positions 0 to lengths[r] - 1; some request has exactly 1024.
All inputs are finite; a program needn't handle non-finite values.
Results may differ from the reference program's by a relative error of at most 0.015.
Values may be sent and summed in bfloat16 or wider, within the bound.
A program may use at most 128 MiB of HBM per device.

```python
import math
import jax
import jax.numpy as jnp
import numpy as np
from jax import lax

D = 2560
QUERY_HEADS = 20
KEY_VALUE_HEADS = 4
HEAD_SIZE = 128
FF = 1536
TOPK = 6
TOK_DEV = 128
EXPERTS = 16
CAP = 64
TOKENS = 4096
REQUEST_COUNT = 32
CACHE_SLOTS = 1024
N_EP = 32


def shared_plan(key):
    lengths = jax.random.randint(jax.random.fold_in(key, 1), (REQUEST_COUNT,), 1, CACHE_SLOTS + 1)
    longest = jax.random.randint(jax.random.fold_in(key, 3), (), 0, REQUEST_COUNT)
    lengths = jnp.where(jnp.arange(REQUEST_COUNT) == longest, CACHE_SLOTS, lengths).astype(jnp.int32)
    return lengths


def draw_lengths(key, part):
    return shared_plan(key)


def draw_queries(key, part):
    offset_start = jax.random.normal(jax.random.fold_in(key, 5), (REQUEST_COUNT, QUERY_HEADS * HEAD_SIZE), jnp.float32)
    return offset_start.astype(jnp.bfloat16)


def draw_key_cache(key, part):
    offset_start = jax.random.normal(jax.random.fold_in(key, 6), (REQUEST_COUNT, CACHE_SLOTS, KEY_VALUE_HEADS * HEAD_SIZE), jnp.float32)
    return offset_start.astype(jnp.bfloat16)


def steps_of(key, shape, split, low, largest):
    def one(dim, blocks):
        heights = jax.random.uniform(jax.random.fold_in(jax.random.fold_in(key, 6), dim), (blocks,), jnp.float32, low / len(split), largest / len(split))
        return jnp.repeat(jnp.exp(heights), shape[dim] // blocks).reshape((-1,) + (1,) * (len(shape) - dim - 1))

    loudness = one(*split[0])
    for cut in split[1:]:
        loudness = loudness * one(*cut)
    return loudness


def routed_block(stream_key, own, number, rows, number_of, top, reach, skew):
    order = jax.random.permutation(stream_key, number_of)
    heavy_load, common = shares(number_of, rows * top, reach, skew, True), shares(number_of, rows * top, reach, skew, False)
    places = jnp.arange(number_of)

    def named(tallies, turn):
        used = int((tallies > 0).sum())
        fixed = max(1, used // 4)
        passed = fixed + (places - fixed + turn * (used - fixed)) % max(1, number_of - fixed)
        return jnp.zeros((number_of,), jnp.int32).at[order[jnp.where(places < fixed, places, passed)]].set(jnp.asarray(tallies, jnp.int32))

    tallies = jnp.where(number % 4 == 0, named(heavy_load, number // 4), named(common, number - number // 4 - 1))
    mixed = jax.random.permutation(jax.random.fold_in(own, 3), number_of)
    giver, taker = mixed[0:number_of // 2 * 2:2], mixed[1:number_of // 2 * 2:2]
    room = jnp.minimum(tallies[giver] - 1, reach - tallies[taker]) // 2
    room = jnp.where((giver == order[0]) | (taker == order[0]) | (tallies[taker] == 0), 0, jnp.maximum(room, 0))
    passed = jax.random.randint(jax.random.fold_in(own, 4), (number_of // 2,), 0, 1 << 20) % (room + 1)
    tallies = tallies.at[giver].add(-passed).at[taker].add(passed)
    items = jnp.searchsorted(jnp.cumsum(tallies), jnp.arange(rows * top), side="right").astype(jnp.int32)
    table = items.reshape(top, rows).T
    table = table[jax.random.permutation(jax.random.fold_in(own, 1), rows)]
    turn = jax.random.randint(jax.random.fold_in(own, 2), (rows, 1), 0, top)
    return jnp.take_along_axis(table, (jnp.arange(top)[None, :] + turn) % top, axis=1)


def shares(amount, total, limit, lean, full):
    portions = [(1 << 20) // math.isqrt(grade ** lean) + 1 for grade in range(1, amount + 1)]
    largest = limit if full else min(limit, max(-(-total // amount), total * portions[0] // sum(portions)))
    least = 1 if total - largest >= amount - 1 else 0
    holding, surplus = [largest] + [least] * (amount - 1), total - largest - least * (amount - 1)
    while surplus > 0:
        free = [i for i in range(1, amount) if holding[i] < largest] or [i for i in range(1, amount) if holding[i] < limit]
        pool, left = sum([portions[i] for i in free]), surplus
        for i in free:
            extra = min(limit - holding[i], max(1, left * portions[i] // pool), surplus)
            holding[i] = holding[i] + extra
            surplus = surplus - extra
    return np.array(holding)


def bell_draw(stream_key, extent, scale, most, cuts=(), held_as=jnp.bfloat16):
    drawn = scale * jax.random.normal(stream_key, extent, jnp.float32)
    if cuts:
        drawn = drawn * steps_of(stream_key, extent, cuts, -0.22, 0.18)
    return jnp.clip(drawn, -most, most).astype(held_as)


def setup_inputs(seed: int = 0) -> dict:
    splits = jax.random.split(jax.random.key(seed), 11)
    tokens = bell_draw(splits[0], (TOKENS, D), 1.0, 6.0, ((0, 32),))
    routes_keys = jax.random.split(jax.random.fold_in(splits[1], 1), TOKENS // TOK_DEV)
    routes_turns = jax.random.permutation(jax.random.fold_in(splits[1], 3), TOKENS // TOK_DEV)
    routes = jax.vmap(lambda own, number: routed_block(jax.random.fold_in(splits[1], 2), own, number, TOK_DEV, EXPERTS, TOPK, CAP, 2))(routes_keys, routes_turns).reshape((TOKENS, TOPK))
    route_weights = jnp.clip(0.05 + 0.35 * jax.random.uniform(splits[2], (TOKENS, TOPK), jnp.float32) ** steps_of(splits[2], (TOKENS, TOPK), ((0, 32),), -0.2, 0.2), 0.05, 0.4)
    w_gate = bell_draw(splits[3], (2 * EXPERTS, D, FF // 2), D ** -0.5, 0.125, ((0, 32),))
    w_up = bell_draw(splits[4], (2 * EXPERTS, D, FF // 2), D ** -0.5, 0.125, ((0, 32),))
    w_down = bell_draw(splits[5], (2 * EXPERTS, FF // 2, D), FF ** -0.5, 0.15625, ((0, 32),))
    queries = draw_queries(jax.random.fold_in(splits[10], 71), 0)
    key_cache = draw_key_cache(jax.random.fold_in(splits[10], 71), 0)
    value_cache = bell_draw(splits[8], (REQUEST_COUNT, CACHE_SLOTS, KEY_VALUE_HEADS * HEAD_SIZE), 1.0, 6.0, ((0, 32),))
    lengths = draw_lengths(jax.random.fold_in(splits[10], 71), 0)
    return {"tokens": tokens, "routes": routes, "route_weights": route_weights, "w_gate": w_gate, "w_up": w_up, "w_down": w_down, "queries": queries, "key_cache": key_cache, "value_cache": value_cache, "lengths": lengths}


floor_score = -1e+30

def route_slots(routes):
    per_device = routes.reshape(N_EP, TOK_DEV * TOPK)
    onehot = (per_device[:, :, None] == jnp.arange(EXPERTS, dtype=jnp.int32)[None, None, :]).astype(jnp.int32)
    before = jnp.cumsum(onehot, axis=1) - onehot
    return lax.optimization_barrier(jnp.sum(before * onehot, axis=2)).astype(jnp.int32)

def expert_block(tokens, routes, route_weights, w_gate, w_up, w_down):
    slots = route_slots(routes)
    source = jnp.arange(N_EP, dtype=jnp.int32)[:, None]
    chosen = routes.reshape(N_EP, TOK_DEV * TOPK).astype(jnp.int32)
    place = (chosen * (N_EP * CAP) + source * CAP + slots).reshape(-1).astype(jnp.int32)
    owner = (jnp.arange(TOKENS * TOPK, dtype=jnp.int32) // TOPK).astype(jnp.int32)
    table = jnp.full((EXPERTS * N_EP * CAP,), TOKENS, jnp.int32).at[place].set(owner)
    table = table.reshape(EXPERTS, N_EP * CAP)
    scales = jnp.zeros((EXPERTS * N_EP * CAP,), jnp.float32).at[place].set(route_weights.reshape(-1))
    scales = scales.reshape(EXPERTS, N_EP * CAP)
    padded = jnp.concatenate([tokens, jnp.zeros((1, D), tokens.dtype)], axis=0)

    def one_expert(carry, expert):
        rows = padded[table[expert]]
        gate_whole = jnp.concatenate([w_gate[2 * expert], w_gate[2 * expert + 1]], axis=1)
        up_whole = jnp.concatenate([w_up[2 * expert], w_up[2 * expert + 1]], axis=1)
        gate_act = jnp.dot(rows, gate_whole, preferred_element_type=jnp.float32)
        up_act = jnp.dot(rows, up_whole, preferred_element_type=jnp.float32)
        hidden = (jax.nn.silu(gate_act) * up_act).astype(jnp.bfloat16)
        result = jnp.zeros((N_EP * CAP, D), jnp.float32)
        for half in range(2):
            start = half * (FF // 2)
            piece = hidden[:, start:start + FF // 2]
            term = jnp.dot(piece, w_down[2 * expert + half], preferred_element_type=jnp.float32).astype(jnp.bfloat16)
            result = result + lax.optimization_barrier(term).astype(jnp.float32)
        carry = carry.at[table[expert]].add(scales[expert][:, None] * result)
        return (carry, None)
    total, _ = lax.scan(one_expert, jnp.zeros((TOKENS + 1, D), jnp.float32), jnp.arange(EXPERTS, dtype=jnp.int32))
    return total[:TOKENS].astype(jnp.bfloat16)

def attention(queries, key_cache, value_cache, lengths):
    scale = 1.0 / math.sqrt(HEAD_SIZE)

    def one_request(item):
        query_vector, key_rows, value_rows, length = item
        heads_of_queries = query_vector.reshape(KEY_VALUE_HEADS, QUERY_HEADS // KEY_VALUE_HEADS, HEAD_SIZE).astype(jnp.float32)
        heads_of_keys = key_rows.reshape(CACHE_SLOTS, KEY_VALUE_HEADS, HEAD_SIZE).astype(jnp.float32)
        heads_of_values = value_rows.reshape(CACHE_SLOTS, KEY_VALUE_HEADS, HEAD_SIZE).astype(jnp.float32)
        scores = jnp.einsum('gjd,cgd->gjc', heads_of_queries, heads_of_keys) * scale
        valid = (jnp.arange(CACHE_SLOTS, dtype=jnp.int32) < length)[None, None, :]
        scores = jnp.where(valid, scores, floor_score)
        top = lax.optimization_barrier(jnp.max(scores, axis=-1, keepdims=True))
        weights = jnp.where(valid, jnp.exp(scores - top), 0.0)
        total = lax.optimization_barrier(jnp.sum(weights, axis=-1))
        rounded = lax.optimization_barrier(weights.astype(jnp.bfloat16)).astype(jnp.float32)
        mixed = jnp.einsum('gjc,cgd->gjd', rounded, heads_of_values)
        return (mixed / total[..., None]).reshape(QUERY_HEADS * HEAD_SIZE).astype(jnp.bfloat16)
    return lax.map(one_request, (queries, key_cache, value_cache, lengths))

def reference(tokens, routes, route_weights, w_gate, w_up, w_down, queries, key_cache, value_cache, lengths):
    moe_out = expert_block(tokens, routes, route_weights, w_gate, w_up, w_down)
    attn_out = attention(queries, key_cache, value_cache, lengths)
    return (moe_out, attn_out)
```

```python
import math

import jax
import jax.numpy as jnp
from jax import lax
from jax.sharding import PartitionSpec as P

QUERY_HEADS = 20
KEY_VALUE_HEADS = 4
HEAD_SIZE = 128


floor_score = -1e30


def attend(queries, key_cache, value_cache, lengths):
    request_list = queries.shape[0]
    window_length = key_cache.shape[1]
    heads_of_queries = queries.reshape(
        request_list, KEY_VALUE_HEADS, QUERY_HEADS // KEY_VALUE_HEADS, HEAD_SIZE
    )
    heads_of_keys = key_cache.reshape(request_list, window_length, KEY_VALUE_HEADS, HEAD_SIZE)
    heads_of_values = value_cache.reshape(request_list, window_length, KEY_VALUE_HEADS, HEAD_SIZE)
    scores = jnp.einsum(
        "rgjd,rcgd->rgjc", heads_of_queries, heads_of_keys, preferred_element_type=jnp.float32
    )
    scores = scores * (1.0 / math.sqrt(HEAD_SIZE))
    position = lax.axis_index("kv") * window_length + jnp.arange(window_length, dtype=jnp.int32)
    valid = (position[None, :] < lengths[:, None])[:, None, None, :]
    scores = jnp.where(valid, scores, floor_score)
    top = lax.pmax(jnp.max(scores, axis=-1), "kv")
    weights = jnp.where(valid, jnp.exp(scores - top[..., None]), 0.0)
    local_total = jnp.sum(weights, axis=-1)
    local_mixed = jnp.einsum(
        "rgjc,rcgd->rgjd",
        weights.astype(jnp.bfloat16),
        heads_of_values,
        preferred_element_type=jnp.float32,
    )
    total, mixed = lax.psum((local_total, local_mixed), "kv")
    return (
        (mixed / total[..., None])
        .reshape(request_list, QUERY_HEADS * HEAD_SIZE)
        .astype(jnp.bfloat16)
    )


def expert_math(flat_rows, gate_part, up_part, down_part):
    gate_act = jnp.dot(flat_rows, gate_part, preferred_element_type=jnp.float32)
    up_act = jnp.dot(flat_rows, up_part, preferred_element_type=jnp.float32)
    hidden = (jax.nn.silu(gate_act) * up_act).astype(jnp.bfloat16)
    return jnp.dot(hidden, down_part, preferred_element_type=jnp.float32)


def expert_gathered(tokens, routes, route_weights, w_gate, w_up, w_down):
    tok, width = tokens.shape
    topk = routes.shape[1]
    halves = lax.axis_size("ep")
    cap = tok * topk * 4 // (3 * (halves // 2))
    expert = lax.axis_index("ep") // 2
    plan = jnp.concatenate([routes.astype(jnp.float32), route_weights], axis=1)
    plans = lax.all_gather(plan, "ep", axis=0)
    gathered = lax.all_gather(tokens, "ep", axis=0)
    match = plans[:, :, :topk] == expert.astype(jnp.float32)
    routed = jnp.any(match, axis=2)
    factor = jnp.sum(jnp.where(match, plans[:, :, topk:], 0.0), axis=2)
    earlier = jnp.triu(jnp.ones((tok, tok), jnp.bfloat16), 1)
    slot = jnp.dot(routed.astype(jnp.bfloat16), earlier, preferred_element_type=jnp.float32)
    slot = jnp.where(routed, slot.astype(jnp.int32), -1)
    chosen = slot[:, None, :] == jnp.arange(cap, dtype=jnp.int32)[None, :, None]
    pick = chosen.astype(jnp.bfloat16)
    scale = jnp.sum(jnp.where(chosen, factor[:, None, :], 0.0), axis=2)
    rows = jnp.einsum("bst,btd->bsd", pick, gathered, preferred_element_type=jnp.float32)
    rows = rows.astype(jnp.bfloat16).reshape(halves * cap, width)
    half_out = expert_math(rows, w_gate[0], w_up[0], w_down[0])
    weighted = (half_out.reshape(halves, cap, width) * scale[:, :, None]).astype(jnp.bfloat16)
    spread = jnp.einsum("bst,bsd->btd", pick, weighted, preferred_element_type=jnp.float32)
    spread = spread.astype(jnp.bfloat16).reshape(halves * tok, width)
    return lax.psum_scatter(spread, "ep", scatter_dimension=0, tiled=True)


def shards(
    tokens, routes, route_weights, w_gate, w_up, w_down, queries, key_cache, value_cache, lengths
):
    if lax.axis_size("kv") == 1:
        moe_out = expert_gathered(tokens, routes, route_weights, w_gate, w_up, w_down)
        return (moe_out, attend(queries, key_cache, value_cache, lengths))
    tok = tokens.shape[0]
    width = tokens.shape[1]
    topk = routes.shape[1]
    halves = lax.axis_size("ep")
    shares = lax.axis_size("kv")
    experts = halves // 2
    cap = tok * topk * 4 // (3 * experts)
    share_cap = cap // shares
    kv_index = lax.axis_index("kv")
    chosen = routes.reshape(-1)
    onehot = (chosen[:, None] == jnp.arange(experts, dtype=jnp.int32)[None, :]).astype(jnp.int32)
    before = jnp.cumsum(onehot, axis=0) - onehot
    slot = jnp.sum(before * onehot, axis=1)
    owner = jnp.arange(tok * topk, dtype=jnp.int32) // topk
    pick = jnp.full((experts * cap,), tok, jnp.int32).at[chosen * cap + slot].set(owner)
    padded = jnp.concatenate([tokens, jnp.zeros((1, width), tokens.dtype)], axis=0)
    outgoing = padded[pick].reshape(experts, cap, width)
    arrived = lax.all_to_all(
        jnp.repeat(outgoing, 2, axis=0), "ep", split_axis=0, concat_axis=0, tiled=True
    )
    flat_rows = arrived.reshape(halves * cap, width)
    partial_out = expert_math(flat_rows, w_gate[0], w_up[0], w_down[0]).reshape(halves, cap, width)
    half_out = lax.psum_scatter(
        partial_out.astype(jnp.bfloat16), "kv", scatter_dimension=1, tiled=True
    )
    back = lax.all_to_all(half_out, "ep", split_axis=0, concat_axis=0, tiled=True)
    table = back.reshape(halves * share_cap, width)
    local_slot = slot - kv_index * share_cap
    held = (local_slot >= 0) & (local_slot < share_cap)
    safe_slot = jnp.where(held, local_slot, 0)
    first_row = 2 * chosen * share_cap + safe_slot
    both = table[first_row].astype(jnp.float32) + table[first_row + share_cap].astype(jnp.float32)
    factor = jnp.where(held, route_weights.reshape(-1), 0.0)
    weighted = both * factor[:, None]
    summed = jnp.sum(weighted.reshape(tok, topk, width), axis=1)
    moe_out = lax.psum(summed.astype(jnp.bfloat16), "kv")
    attn_out = attend(queries, key_cache, value_cache, lengths)
    return (moe_out, attn_out)


def solution(mesh):
    return jax.shard_map(
        shards,
        mesh=mesh,
        in_specs=(
            P("ep", None),
            P("ep", None),
            P("ep", None),
            P("ep", None, "kv"),
            P("ep", None, "kv"),
            P("ep", "kv", None),
            P("ep", None),
            P("ep", "kv", None),
            P("ep", "kv", None),
            P("ep"),
        ),
        out_specs=(P("ep", None), P("ep", None)),
        check_vma=False,
    )
```

```python
import functools
import math

import jax
import jax.numpy as jnp
from jax import lax
from jax.experimental import pallas as pl
from jax.experimental.pallas import tpu as pltpu
from jax.sharding import PartitionSpec as P

QUERY_HEADS = 20
KEY_VALUE_HEADS = 4
HEAD_SIZE = 128


floor_score = -1e30


def attend(queries, key_cache, value_cache, lengths):
    request_list = queries.shape[0]
    window_length = key_cache.shape[1]
    heads_of_queries = queries.reshape(
        request_list, KEY_VALUE_HEADS, QUERY_HEADS // KEY_VALUE_HEADS, HEAD_SIZE
    )
    heads_of_keys = key_cache.reshape(request_list, window_length, KEY_VALUE_HEADS, HEAD_SIZE)
    heads_of_values = value_cache.reshape(request_list, window_length, KEY_VALUE_HEADS, HEAD_SIZE)
    scores = jnp.einsum(
        "rgjd,rcgd->rgjc", heads_of_queries, heads_of_keys, preferred_element_type=jnp.float32
    )
    scores = scores * (1.0 / math.sqrt(HEAD_SIZE))
    position = lax.axis_index("kv") * window_length + jnp.arange(window_length, dtype=jnp.int32)
    valid = (position[None, :] < lengths[:, None])[:, None, None, :]
    scores = jnp.where(valid, scores, floor_score)
    top = lax.pmax(jnp.max(scores, axis=-1), "kv")
    weights = jnp.where(valid, jnp.exp(scores - top[..., None]), 0.0)
    local_total = jnp.sum(weights, axis=-1)
    local_mixed = jnp.einsum(
        "rgjc,rcgd->rgjd",
        weights.astype(jnp.bfloat16),
        heads_of_values,
        preferred_element_type=jnp.float32,
    )
    total, mixed = lax.psum((local_total, local_mixed), "kv")
    return (
        (mixed / total[..., None])
        .reshape(request_list, QUERY_HEADS * HEAD_SIZE)
        .astype(jnp.bfloat16)
    )


def expert_math(flat_rows, gate_part, up_part, down_part):
    gate_act = jnp.dot(flat_rows, gate_part, preferred_element_type=jnp.float32)
    up_act = jnp.dot(flat_rows, up_part, preferred_element_type=jnp.float32)
    hidden = (jax.nn.silu(gate_act) * up_act).astype(jnp.bfloat16)
    return jnp.dot(hidden, down_part, preferred_element_type=jnp.float32)


MESH = pl.DeviceIdType.MESH
PLANE = ((0, 0), (1, 0), (0, 1), (1, 1))


def place(nz):
    me = lax.axis_index("ep")
    return me // 8, (me // 4) % 2, (me // 2) % 2, me % 2


def index_of(z, y, x, core):
    return ((z * 2 + y) * 2 + x) * 2 + core


def flip(value, bit):
    return 1 - value if bit else value


def greet(peers):
    barrier = pltpu.get_barrier_semaphore()
    for peer in peers:
        pl.semaphore_signal(barrier, inc=1, device_id={"ep": peer}, device_id_type=MESH)
    pl.semaphore_wait(barrier, len(peers))


def push(src, dst, send_sem, recv_sem, peer):
    copy = pltpu.make_async_remote_copy(
        src_ref=src,
        dst_ref=dst,
        send_sem=send_sem,
        recv_sem=recv_sem,
        device_id={"ep": peer},
        device_id_type=MESH,
    )
    copy.start()
    return copy


def neighbours(nz):
    z, y, x, core = place(nz)
    plane = [index_of(z, flip(y, dy), flip(x, dx), core) for dx, dy in PLANE]
    partner = index_of(z, y, x, 1 - core)
    ahead = [index_of((z + step) % nz, y, x, core) for step in range(nz)]
    behind = [index_of((z + nz - step) % nz, y, x, core) for step in range(nz)]
    experts = [(z * 2 + flip(y, dy)) * 2 + flip(x, dx) for dx, dy in PLANE]
    return plane, partner, ahead, behind, experts


def arrival_order(nz):
    return [0] + sorted(range(1, nz), key=lambda step: min(step, nz - step))


def dispatch_kernel(
    nz, cap, tokens, plan, rows, plans, line, picked,
    line_send, line_recv, plan_send, plan_recv, plane_send, plane_recv, core_send, core_recv,
):
    plane, partner, ahead, behind, experts = neighbours(nz)
    tok = tokens.shape[0]
    greet(plane[1:] + [partner] + ahead[1:])
    line_copies, plan_copies = [None] * nz, [None] * nz
    for step in arrival_order(nz)[1:]:
        plan_copies[step] = push(
            plan, plans.at[step], plan_send.at[step], plan_recv.at[step], ahead[step]
        )
        line_copies[step] = push(
            tokens, line.at[step], line_send.at[step], line_recv.at[step], ahead[step]
        )
    plans[0] = plan[...]
    row_of = lax.broadcasted_iota(jnp.int32, (cap, tok), 0).astype(jnp.float32)
    plane_copies, core_copies, local_copies = {}, {}, []

    def forward(step):
        for p in range(1, 4):
            plane_copies[p, step].wait_recv()
            core_copies[p, step] = push(
                rows.at[0, p, step], rows.at[1, p, step],
                core_send.at[p, step], core_recv.at[p, step], partner,
            )

    last = None
    for step in arrival_order(nz):
        if step:
            plan_copies[step].wait_recv()
            line_copies[step].wait_recv()
        block = line.at[step] if step else tokens
        for p in (3, 1, 2, 0):
            slots = plans[step, pl.ds(experts[p], 1), :]
            pick = jnp.where(row_of == slots, 1.0, 0.0).astype(jnp.bfloat16)
            picked[p, step] = jnp.dot(
                pick, block[...], preferred_element_type=jnp.float32
            ).astype(jnp.bfloat16)
            if p:
                plane_copies[p, step] = push(
                    picked.at[p, step], rows.at[0, p, step],
                    plane_send.at[p, step], plane_recv.at[p, step], plane[p],
                )
            else:
                core_copies[p, step] = push(
                    picked.at[p, step], rows.at[1, p, step],
                    core_send.at[p, step], core_recv.at[p, step], partner,
                )
                copy = pltpu.make_async_copy(
                    picked.at[p, step], rows.at[0, p, step], plane_send.at[p, step]
                )
                copy.start()
                local_copies.append(copy)
        if last is not None:
            forward(last)
        last = step
    forward(last)
    for copy in local_copies:
        copy.wait()
    for copy in plan_copies[1:] + line_copies[1:] + list(plane_copies.values()):
        copy.wait_send()
    for copy in core_copies.values():
        copy.wait()


def combine_kernel(
    nz, cap, half_out, plans, out, own, other, back, partial, sums,
    own_sem, core_send, core_recv, plane_send, plane_recv, line_send, line_recv,
):
    plane, partner, ahead, behind, experts = neighbours(nz)
    tok = out.shape[0]
    greet(plane[1:] + [partner] + behind[1:])
    order = arrival_order(nz)[1:][::-1] + [0]
    core_copies, own_copies, plane_copies, line_copies = {}, {}, {}, {}
    for step in order:
        for p in (3, 1, 2, 0):
            core_copies[p, step] = push(
                half_out.at[1, p, step], other.at[p, step],
                core_send.at[p, step], core_recv.at[p, step], partner,
            )
            own_copies[p, step] = pltpu.make_async_copy(
                half_out.at[0, p, step], own.at[p, step], own_sem.at[p, step]
            )
            own_copies[p, step].start()
    for step in order:
        for p in (3, 1, 2, 0):
            core_copies[p, step].wait_recv()
            own_copies[p, step].wait()
            both = own[p, step].astype(jnp.float32) + other[p, step].astype(jnp.float32)
            sums[p, step] = both.astype(jnp.bfloat16)
            if p:
                plane_copies[p, step] = push(
                    sums.at[p, step], back.at[p, step],
                    plane_send.at[p, step], plane_recv.at[p, step], plane[p],
                )
    row_of = lax.broadcasted_iota(jnp.int32, (cap, tok), 0).astype(jnp.float32)
    total = None
    for step in order:
        total = jnp.zeros((tok, out.shape[1]), jnp.float32)
        for p in (0, 2, 1, 3):
            if p:
                plane_copies[p, step].wait_recv()
            slots = plans[step, pl.ds(experts[p], 1), :]
            factors = plans[step, pl.ds(experts[p] + 4 * nz, 1), :]
            spread = jnp.where(row_of == slots, factors, 0.0).T
            high = spread.astype(jnp.bfloat16)
            low = (spread - high.astype(jnp.float32)).astype(jnp.bfloat16)
            values = back[p, step] if p else sums[p, step]
            total += jnp.dot(high, values, preferred_element_type=jnp.float32)
            total += jnp.dot(low, values, preferred_element_type=jnp.float32)
        if step:
            partial[0, step] = total.astype(jnp.bfloat16)
            line_copies[step] = push(
                partial.at[0, step], partial.at[1, step],
                line_send.at[step], line_recv.at[step], behind[step],
            )
    for step in order[:-1]:
        line_copies[step].wait_recv()
        total += partial[1, step].astype(jnp.float32)
    out[...] = total.astype(out.dtype)
    for copies in (core_copies, plane_copies, line_copies):
        for copy in copies.values():
            copy.wait_send()


def expert_lines(tokens, routes, route_weights, w_gate, w_up, w_down):
    tok, width = tokens.shape
    topk = routes.shape[1]
    halves = lax.axis_size("ep")
    experts = halves // 2
    nz = halves // 8
    cap = tok * topk * 4 // (3 * experts)
    match = routes[None, :, :] == jnp.arange(experts, dtype=jnp.int32)[:, None, None]
    routed = jnp.any(match, axis=2)
    factor = jnp.sum(jnp.where(match, route_weights[None, :, :], 0.0), axis=2)
    earlier = jnp.triu(jnp.ones((tok, tok), jnp.bfloat16), 1)
    slot = jnp.dot(routed.astype(jnp.bfloat16), earlier, preferred_element_type=jnp.float32)
    plan = jnp.concatenate([jnp.where(routed, slot, -1.0), factor], axis=0)
    vmem, anywhere = pl.BlockSpec(memory_space=pltpu.VMEM), pl.BlockSpec(memory_space=pl.ANY)
    dma = pltpu.SemaphoreType.DMA
    rows, plans = pl.pallas_call(
        functools.partial(dispatch_kernel, nz, cap),
        out_shape=(
            jax.ShapeDtypeStruct((2, 4, nz, cap, width), jnp.bfloat16),
            jax.ShapeDtypeStruct((nz, 2 * experts, tok), jnp.float32),
        ),
        in_specs=[vmem, vmem],
        out_specs=(anywhere, vmem),
        scratch_shapes=[
            pltpu.VMEM((nz, tok, width), jnp.bfloat16),
            pltpu.VMEM((4, nz, cap, width), jnp.bfloat16),
            dma((nz,)), dma((nz,)), dma((nz,)), dma((nz,)),
            dma((4, nz)), dma((4, nz)), dma((4, nz)), dma((4, nz)),
        ],
        compiler_params=pltpu.CompilerParams(
            collective_id=0, has_side_effects=True, vmem_limit_bytes=40 << 20
        ),
    )(tokens, plan)
    half_out = expert_math(rows.reshape(halves * cap, width), w_gate[0], w_up[0], w_down[0])
    half_out = half_out.astype(jnp.bfloat16).reshape(2, 4, nz, cap, width)
    return pl.pallas_call(
        functools.partial(combine_kernel, nz, cap),
        out_shape=jax.ShapeDtypeStruct((tok, width), jnp.bfloat16),
        in_specs=[anywhere, vmem],
        out_specs=vmem,
        scratch_shapes=[
            pltpu.VMEM((4, nz, cap, width), jnp.bfloat16),
            pltpu.VMEM((4, nz, cap, width), jnp.bfloat16),
            pltpu.VMEM((4, nz, cap, width), jnp.bfloat16),
            pltpu.VMEM((2, nz, tok, width), jnp.bfloat16),
            pltpu.VMEM((4, nz, cap, width), jnp.bfloat16),
            dma((4, nz)), dma((4, nz)), dma((4, nz)), dma((4, nz)), dma((4, nz)),
            dma((nz,)), dma((nz,)),
        ],
        compiler_params=pltpu.CompilerParams(
            collective_id=1, has_side_effects=True, vmem_limit_bytes=48 << 20
        ),
    )(half_out, plans)


def shards(
    tokens, routes, route_weights, w_gate, w_up, w_down, queries, key_cache, value_cache, lengths
):
    if lax.axis_size("kv") == 1:
        moe_out = expert_lines(tokens, routes, route_weights, w_gate, w_up, w_down)
        return (moe_out, attend(queries, key_cache, value_cache, lengths))
    tok = tokens.shape[0]
    width = tokens.shape[1]
    topk = routes.shape[1]
    halves = lax.axis_size("ep")
    shares = lax.axis_size("kv")
    experts = halves // 2
    cap = tok * topk * 4 // (3 * experts)
    share_cap = cap // shares
    kv_index = lax.axis_index("kv")
    chosen = routes.reshape(-1)
    onehot = (chosen[:, None] == jnp.arange(experts, dtype=jnp.int32)[None, :]).astype(jnp.int32)
    before = jnp.cumsum(onehot, axis=0) - onehot
    slot = jnp.sum(before * onehot, axis=1)
    owner = jnp.arange(tok * topk, dtype=jnp.int32) // topk
    pick = jnp.full((experts * cap,), tok, jnp.int32).at[chosen * cap + slot].set(owner)
    padded = jnp.concatenate([tokens, jnp.zeros((1, width), tokens.dtype)], axis=0)
    outgoing = padded[pick].reshape(experts, cap, width)
    arrived = lax.all_to_all(
        jnp.repeat(outgoing, 2, axis=0), "ep", split_axis=0, concat_axis=0, tiled=True
    )
    flat_rows = arrived.reshape(halves * cap, width)
    partial_out = expert_math(flat_rows, w_gate[0], w_up[0], w_down[0]).reshape(halves, cap, width)
    half_out = lax.psum_scatter(
        partial_out.astype(jnp.bfloat16), "kv", scatter_dimension=1, tiled=True
    )
    back = lax.all_to_all(half_out, "ep", split_axis=0, concat_axis=0, tiled=True)
    table = back.reshape(halves * share_cap, width)
    local_slot = slot - kv_index * share_cap
    held = (local_slot >= 0) & (local_slot < share_cap)
    safe_slot = jnp.where(held, local_slot, 0)
    first_row = 2 * chosen * share_cap + safe_slot
    both = table[first_row].astype(jnp.float32) + table[first_row + share_cap].astype(jnp.float32)
    factor = jnp.where(held, route_weights.reshape(-1), 0.0)
    weighted = both * factor[:, None]
    summed = jnp.sum(weighted.reshape(tok, topk, width), axis=1)
    moe_out = lax.psum(summed.astype(jnp.bfloat16), "kv")
    attn_out = attend(queries, key_cache, value_cache, lengths)
    return (moe_out, attn_out)


def solution(mesh):
    return jax.shard_map(
        shards,
        mesh=mesh,
        in_specs=(
            P("ep", None),
            P("ep", None),
            P("ep", None),
            P("ep", None, "kv"),
            P("ep", None, "kv"),
            P("ep", "kv", None),
            P("ep", None),
            P("ep", "kv", None),
            P("ep", "kv", None),
            P("ep"),
        ),
        out_specs=(P("ep", None), P("ep", None)),
        check_vma=False,
    )
```

```python
import functools
import math

import jax
import jax.numpy as jnp
from jax import lax
from jax.experimental import pallas as pl
from jax.experimental.pallas import tpu as pltpu
from jax.sharding import PartitionSpec as P

QUERY_HEADS = 20
KEY_VALUE_HEADS = 4
HEAD_SIZE = 128


floor_score = -1e30


def attend(queries, key_cache, value_cache, lengths):
    request_list = queries.shape[0]
    window_length = key_cache.shape[1]
    heads_of_queries = queries.reshape(
        request_list, KEY_VALUE_HEADS, QUERY_HEADS // KEY_VALUE_HEADS, HEAD_SIZE
    )
    heads_of_keys = key_cache.reshape(request_list, window_length, KEY_VALUE_HEADS, HEAD_SIZE)
    heads_of_values = value_cache.reshape(request_list, window_length, KEY_VALUE_HEADS, HEAD_SIZE)
    scores = jnp.einsum(
        "rgjd,rcgd->rgjc", heads_of_queries, heads_of_keys, preferred_element_type=jnp.float32
    )
    scores = scores * (1.0 / math.sqrt(HEAD_SIZE))
    position = lax.axis_index("kv") * window_length + jnp.arange(window_length, dtype=jnp.int32)
    valid = (position[None, :] < lengths[:, None])[:, None, None, :]
    scores = jnp.where(valid, scores, floor_score)
    top = lax.pmax(jnp.max(scores, axis=-1), "kv")
    weights = jnp.where(valid, jnp.exp(scores - top[..., None]), 0.0)
    local_total = jnp.sum(weights, axis=-1)
    local_mixed = jnp.einsum(
        "rgjc,rcgd->rgjd",
        weights.astype(jnp.bfloat16),
        heads_of_values,
        preferred_element_type=jnp.float32,
    )
    total, mixed = lax.psum((local_total, local_mixed), "kv")
    return (
        (mixed / total[..., None])
        .reshape(request_list, QUERY_HEADS * HEAD_SIZE)
        .astype(jnp.bfloat16)
    )


def expert_math(flat_rows, gate_part, up_part, down_part):
    gate_act = jnp.dot(flat_rows, gate_part, preferred_element_type=jnp.float32)
    up_act = jnp.dot(flat_rows, up_part, preferred_element_type=jnp.float32)
    hidden = (jax.nn.silu(gate_act) * up_act).astype(jnp.bfloat16)
    return jnp.dot(hidden, down_part, preferred_element_type=jnp.float32)


MESH = pl.DeviceIdType.MESH
PLANE = ((0, 0), (1, 0), (0, 1), (1, 1))


def place(nz):
    me = lax.axis_index("ep")
    return me // 8, (me // 4) % 2, (me // 2) % 2, me % 2


def index_of(z, y, x, core):
    return ((z * 2 + y) * 2 + x) * 2 + core


def flip(value, bit):
    return 1 - value if bit else value


def greet(peers):
    barrier = pltpu.get_barrier_semaphore()
    for peer in peers:
        pl.semaphore_signal(barrier, inc=1, device_id={"ep": peer}, device_id_type=MESH)
    pl.semaphore_wait(barrier, len(peers))


def push(src, dst, send_sem, recv_sem, peer):
    copy = pltpu.make_async_remote_copy(
        src_ref=src,
        dst_ref=dst,
        send_sem=send_sem,
        recv_sem=recv_sem,
        device_id={"ep": peer},
        device_id_type=MESH,
    )
    copy.start()
    return copy


def neighbours(nz):
    z, y, x, core = place(nz)
    plane = [index_of(z, flip(y, dy), flip(x, dx), core) for dx, dy in PLANE]
    partner = index_of(z, y, x, 1 - core)
    line = [index_of(mirror(z, step), y, x, core) for step in range(nz)]
    experts = [(z * 2 + flip(y, dy)) * 2 + flip(x, dx) for dx, dy in PLANE]
    return plane, partner, line, experts


def mirror(z, step):
    value, unit = 0, 1
    while unit <= step:
        value += unit * flip((z // unit) % 2, (step // unit) % 2)
        unit *= 2
    return value + (z // unit) * unit


def experts_kernel(
    nz, cap, tokens, plan, w_gate, w_up, w_down, out,
    plans, line, picked, rows, hidden, result, other, back, partial, gate_w, up_w, down_w,
    weight_sem, plan_send, plan_recv, line_send, line_recv, plane_send, plane_recv,
    core_send, core_recv, pair_send, pair_recv, back_send, back_recv, home_send, home_recv,
):
    plane, partner, peers, experts = neighbours(nz)
    tok, width = tokens.shape
    units = w_gate.shape[1]
    row_of = lax.broadcasted_iota(jnp.int32, (cap, tok), 0).astype(jnp.float32)
    far = (3, 1, 2)
    copies = {}

    def chunk(core, p):
        return pl.ds((core * 4 + p) * cap, cap)

    def half(core):
        return pl.ds(core * 4 * cap, 4 * cap)

    def spread_line(step):
        copies["plan", step] = push(
            plan, plans.at[step], plan_send.at[step], plan_recv.at[step], peers[step]
        )
        copies["line", step] = push(
            tokens, line.at[step - 1], line_send.at[step], line_recv.at[step], peers[step]
        )

    def dispatch(step):
        if step:
            copies["plan", step].wait_recv()
            copies["line", step].wait_recv()
        block = line.at[step - 1] if step else tokens
        for p in far + (0,):
            slots = plans[step, pl.ds(experts[p], 1), :]
            pick = jnp.where(row_of == slots, 1.0, 0.0).astype(jnp.bfloat16)
            value = jnp.dot(pick, block[...], preferred_element_type=jnp.float32)
            value = value.astype(jnp.bfloat16)
            if p:
                picked[step, p - 1] = value
                copies["plane", step, p] = push(
                    picked.at[step, p - 1], rows.at[step, chunk(0, p)],
                    plane_send.at[step, p], plane_recv.at[step, p], plane[p],
                )
            else:
                rows[step, chunk(0, 0)] = value
                pass_on(step, 0)

    def pass_on(step, p):
        copies["core", step, p] = push(
            rows.at[step, chunk(0, p)], rows.at[step, chunk(1, p)],
            core_send.at[step, p], core_recv.at[step, p], partner,
        )

    def forward(step):
        for p in (1, 2, 3):
            copies["plane", step, p].wait_recv()
            pass_on(step, p)

    def compute(step):
        for p in range(4):
            copies["core", step, p].wait_recv()
        if step == 0:
            for copy in weights:
                copy.wait()
        block = rows.at[step]
        wide = 256

        def first(tile, carry):
            at = pl.ds(pl.multiple_of(tile * wide, wide), wide)
            gate = jnp.dot(block[...], gate_w[:, at], preferred_element_type=jnp.float32)
            up = jnp.dot(block[...], up_w[:, at], preferred_element_type=jnp.float32)
            hidden[:, at] = (gate / (1.0 + jnp.exp(-gate)) * up).astype(jnp.bfloat16)
            return carry

        lax.fori_loop(0, units // wide, first, 0)
        broad = 512

        def second(tile, carry):
            at = pl.ds(pl.multiple_of(tile * broad, broad), broad)
            value = jnp.dot(hidden[...], down_w[:, at], preferred_element_type=jnp.float32)
            result[step, :, at] = value.astype(jnp.bfloat16)
            return carry

        lax.fori_loop(0, width // broad, second, 0)
        copies["pair", step] = push(
            result.at[step, half(1)], other.at[step],
            pair_send.at[step], pair_recv.at[step], partner,
        )

    def finish(step):
        copies["pair", step].wait_recv()
        for p in far + (0,):
            at = pl.ds(p * cap, cap)
            both = result[step, at].astype(jnp.float32) + other[step, at].astype(jnp.float32)
            if p:
                result[step, at] = both.astype(jnp.bfloat16)
                copies["back", step, p] = push(
                    result.at[step, at], back.at[step, at],
                    back_send.at[step, p], back_recv.at[step, p], plane[p],
                )
            else:
                back[step, at] = both.astype(jnp.bfloat16)

    def expand(step):
        spread = []
        for p in range(4):
            if p:
                copies["back", step, p].wait_recv()
            slots = plans[step, pl.ds(experts[p], 1), :]
            factors = plans[step, pl.ds(experts[p] + 4 * nz, 1), :]
            spread.append(jnp.where(row_of == slots, factors, 0.0))
        spread = jnp.concatenate(spread, axis=0).T
        high = spread.astype(jnp.bfloat16)
        low = (spread - high.astype(jnp.float32)).astype(jnp.bfloat16)
        total = jnp.dot(high, back[step], preferred_element_type=jnp.float32)
        total += jnp.dot(low, back[step], preferred_element_type=jnp.float32)
        if step:
            partial[0, step - 1] = total.astype(jnp.bfloat16)
            copies["home", step] = push(
                partial.at[0, step - 1], partial.at[1, step - 1],
                home_send.at[step], home_recv.at[step], peers[step],
            )
        return total

    weights = [
        pltpu.make_async_copy(source, target, weight_sem.at[i])
        for i, (source, target) in enumerate(((w_gate, gate_w), (w_up, up_w), (w_down, down_w)))
    ]
    greet(plane[1:] + [partner] + peers[1:])
    for step in range(1, nz - 1):
        spread_line(step)
    for copy in weights:
        copy.start()
    plans[0] = plan[...]
    dispatch(0)
    forward(0)
    dispatch(1)
    spread_line(nz - 1)
    compute(0)
    forward(1)
    finish(0)
    compute(1)
    for step in range(2, nz):
        dispatch(step)
        finish(step - 1)
        forward(step)
        compute(step)
        expand(step - 1)
    finish(nz - 1)
    expand(nz - 1)
    total = expand(0)
    for step in range(1, nz):
        copies["home", step].wait_recv()
        total += partial[1, step - 1].astype(jnp.float32)
    out[...] = total.astype(out.dtype)
    for copy in copies.values():
        copy.wait_send()


def expert_lines(tokens, routes, route_weights, w_gate, w_up, w_down):
    tok, width = tokens.shape
    topk = routes.shape[1]
    halves = lax.axis_size("ep")
    experts = halves // 2
    nz = halves // 8
    cap = tok * topk * 4 // (3 * experts)
    units = w_gate.shape[2]
    match = routes[None, :, :] == jnp.arange(experts, dtype=jnp.int32)[:, None, None]
    routed = jnp.any(match, axis=2)
    factor = jnp.sum(jnp.where(match, route_weights[None, :, :], 0.0), axis=2)
    earlier = jnp.triu(jnp.ones((tok, tok), jnp.bfloat16), 1)
    slot = jnp.dot(routed.astype(jnp.bfloat16), earlier, preferred_element_type=jnp.float32)
    plan = jnp.concatenate([jnp.where(routed, slot, -1.0), factor], axis=0)
    vmem, anywhere = pl.BlockSpec(memory_space=pltpu.VMEM), pl.BlockSpec(memory_space=pl.ANY)
    dma = pltpu.SemaphoreType.DMA
    half_type = jnp.bfloat16
    return pl.pallas_call(
        functools.partial(experts_kernel, nz, cap),
        out_shape=jax.ShapeDtypeStruct((tok, width), half_type),
        in_specs=[vmem, vmem, anywhere, anywhere, anywhere],
        out_specs=vmem,
        scratch_shapes=[
            pltpu.VMEM((nz, 2 * experts, tok), jnp.float32),
            pltpu.VMEM((nz - 1, tok, width), half_type),
            pltpu.VMEM((nz, 3, cap, width), half_type),
            pltpu.VMEM((nz, 8 * cap, width), half_type),
            pltpu.VMEM((8 * cap, units), half_type),
            pltpu.VMEM((nz, 8 * cap, width), half_type),
            pltpu.VMEM((nz, 4 * cap, width), half_type),
            pltpu.VMEM((nz, 4 * cap, width), half_type),
            pltpu.VMEM((2, nz - 1, tok, width), half_type),
            pltpu.VMEM((width, units), half_type),
            pltpu.VMEM((width, units), half_type),
            pltpu.VMEM((units, width), half_type),
            dma((3,)), dma((nz,)), dma((nz,)), dma((nz,)), dma((nz,)),
            dma((nz, 4)), dma((nz, 4)), dma((nz, 4)), dma((nz, 4)),
            dma((nz,)), dma((nz,)), dma((nz, 4)), dma((nz, 4)), dma((nz,)), dma((nz,)),
        ],
        compiler_params=pltpu.CompilerParams(
            collective_id=0, has_side_effects=True, vmem_limit_bytes=63 << 20
        ),
    )(tokens, plan, w_gate[0], w_up[0], w_down[0])


def shards(
    tokens, routes, route_weights, w_gate, w_up, w_down, queries, key_cache, value_cache, lengths
):
    if lax.axis_size("kv") == 1:
        moe_out = expert_lines(tokens, routes, route_weights, w_gate, w_up, w_down)
        return (moe_out, attend(queries, key_cache, value_cache, lengths))
    tok = tokens.shape[0]
    width = tokens.shape[1]
    topk = routes.shape[1]
    halves = lax.axis_size("ep")
    shares = lax.axis_size("kv")
    experts = halves // 2
    cap = tok * topk * 4 // (3 * experts)
    share_cap = cap // shares
    kv_index = lax.axis_index("kv")
    chosen = routes.reshape(-1)
    onehot = (chosen[:, None] == jnp.arange(experts, dtype=jnp.int32)[None, :]).astype(jnp.int32)
    before = jnp.cumsum(onehot, axis=0) - onehot
    slot = jnp.sum(before * onehot, axis=1)
    owner = jnp.arange(tok * topk, dtype=jnp.int32) // topk
    pick = jnp.full((experts * cap,), tok, jnp.int32).at[chosen * cap + slot].set(owner)
    padded = jnp.concatenate([tokens, jnp.zeros((1, width), tokens.dtype)], axis=0)
    outgoing = padded[pick].reshape(experts, cap, width)
    arrived = lax.all_to_all(
        jnp.repeat(outgoing, 2, axis=0), "ep", split_axis=0, concat_axis=0, tiled=True
    )
    flat_rows = arrived.reshape(halves * cap, width)
    partial_out = expert_math(flat_rows, w_gate[0], w_up[0], w_down[0]).reshape(halves, cap, width)
    half_out = lax.psum_scatter(
        partial_out.astype(jnp.bfloat16), "kv", scatter_dimension=1, tiled=True
    )
    back = lax.all_to_all(half_out, "ep", split_axis=0, concat_axis=0, tiled=True)
    table = back.reshape(halves * share_cap, width)
    local_slot = slot - kv_index * share_cap
    held = (local_slot >= 0) & (local_slot < share_cap)
    safe_slot = jnp.where(held, local_slot, 0)
    first_row = 2 * chosen * share_cap + safe_slot
    both = table[first_row].astype(jnp.float32) + table[first_row + share_cap].astype(jnp.float32)
    factor = jnp.where(held, route_weights.reshape(-1), 0.0)
    weighted = both * factor[:, None]
    summed = jnp.sum(weighted.reshape(tok, topk, width), axis=1)
    moe_out = lax.psum(summed.astype(jnp.bfloat16), "kv")
    attn_out = attend(queries, key_cache, value_cache, lengths)
    return (moe_out, attn_out)


def solution(mesh):
    return jax.shard_map(
        shards,
        mesh=mesh,
        in_specs=(
            P("ep", None),
            P("ep", None),
            P("ep", None),
            P("ep", None, "kv"),
            P("ep", None, "kv"),
            P("ep", "kv", None),
            P("ep", None),
            P("ep", "kv", None),
            P("ep", "kv", None),
            P("ep"),
        ),
        out_specs=(P("ep", None), P("ep", None)),
        check_vma=False,
    )
```

```python
import functools
import math

import jax
import jax.numpy as jnp
from jax import lax
from jax.experimental import pallas as pl
from jax.experimental.pallas import tpu as pltpu
from jax.sharding import PartitionSpec as P

QUERY_HEADS = 20
KEY_VALUE_HEADS = 4
HEAD_SIZE = 128


floor_score = -1e30


def attend(queries, key_cache, value_cache, lengths):
    request_list = queries.shape[0]
    window_length = key_cache.shape[1]
    heads_of_queries = queries.reshape(
        request_list, KEY_VALUE_HEADS, QUERY_HEADS // KEY_VALUE_HEADS, HEAD_SIZE
    )
    heads_of_keys = key_cache.reshape(request_list, window_length, KEY_VALUE_HEADS, HEAD_SIZE)
    heads_of_values = value_cache.reshape(request_list, window_length, KEY_VALUE_HEADS, HEAD_SIZE)
    scores = jnp.einsum(
        "rgjd,rcgd->rgjc", heads_of_queries, heads_of_keys, preferred_element_type=jnp.float32
    )
    scores = scores * (1.0 / math.sqrt(HEAD_SIZE))
    position = lax.axis_index("kv") * window_length + jnp.arange(window_length, dtype=jnp.int32)
    valid = (position[None, :] < lengths[:, None])[:, None, None, :]
    scores = jnp.where(valid, scores, floor_score)
    top = lax.pmax(jnp.max(scores, axis=-1), "kv")
    weights = jnp.where(valid, jnp.exp(scores - top[..., None]), 0.0)
    local_total = jnp.sum(weights, axis=-1)
    local_mixed = jnp.einsum(
        "rgjc,rcgd->rgjd",
        weights.astype(jnp.bfloat16),
        heads_of_values,
        preferred_element_type=jnp.float32,
    )
    total, mixed = lax.psum((local_total, local_mixed), "kv")
    return (
        (mixed / total[..., None])
        .reshape(request_list, QUERY_HEADS * HEAD_SIZE)
        .astype(jnp.bfloat16)
    )


def expert_math(flat_rows, gate_part, up_part, down_part):
    gate_act = jnp.dot(flat_rows, gate_part, preferred_element_type=jnp.float32)
    up_act = jnp.dot(flat_rows, up_part, preferred_element_type=jnp.float32)
    hidden = (jax.nn.silu(gate_act) * up_act).astype(jnp.bfloat16)
    return jnp.dot(hidden, down_part, preferred_element_type=jnp.float32)


MESH = pl.DeviceIdType.MESH
PLANE = ((0, 0), (1, 0), (0, 1), (1, 1))


def place(nz):
    me = lax.axis_index("ep")
    return me // 8, (me // 4) % 2, (me // 2) % 2, me % 2


def index_of(z, y, x, core):
    return ((z * 2 + y) * 2 + x) * 2 + core


def flip(value, bit):
    return 1 - value if bit else value


def greet(peers):
    barrier = pltpu.get_barrier_semaphore()
    for peer in peers:
        pl.semaphore_signal(barrier, inc=1, device_id={"ep": peer}, device_id_type=MESH)
    pl.semaphore_wait(barrier, len(peers))


def push(src, dst, send_sem, recv_sem, peer):
    copy = pltpu.make_async_remote_copy(
        src_ref=src,
        dst_ref=dst,
        send_sem=send_sem,
        recv_sem=recv_sem,
        device_id={"ep": peer},
        device_id_type=MESH,
    )
    copy.start()
    return copy


def neighbours(nz):
    z, y, x, core = place(nz)
    plane = [index_of(z, flip(y, dy), flip(x, dx), core) for dx, dy in PLANE]
    partner = index_of(z, y, x, 1 - core)
    line = [index_of(mirror(z, step), y, x, core) for step in range(nz)]
    experts = [(z * 2 + flip(y, dy)) * 2 + flip(x, dx) for dx, dy in PLANE]
    return plane, partner, line, experts


def mirror(z, step):
    value, unit = 0, 1
    while unit <= step:
        value += unit * flip((z // unit) % 2, (step // unit) % 2)
        unit *= 2
    return value + (z // unit) * unit


def experts_kernel(
    nz, cap, tokens, plan, w_gate, w_up, w_down, out,
    plans, line, picked, rows, hidden, result, other, back, partial, gate_w, up_w, down_w,
    weight_sem, plan_send, plan_recv, line_send, line_recv, plane_send, plane_recv,
    core_send, core_recv, pair_send, pair_recv, back_send, back_recv, home_send, home_recv,
):
    plane, partner, peers, experts = neighbours(nz)
    tok, width = tokens.shape
    units = w_gate.shape[1]
    row_of = lax.broadcasted_iota(jnp.int32, (cap, tok), 0).astype(jnp.float32)
    far = (3, 1, 2)
    copies = {}

    def chunk(core, p):
        return pl.ds((core * 4 + p) * cap, cap)

    def half(core):
        return pl.ds(core * 4 * cap, 4 * cap)

    def spread_line(step):
        copies["plan", step] = push(
            plan, plans.at[step], plan_send.at[step], plan_recv.at[step], peers[step]
        )
        copies["line", step] = push(
            tokens, line.at[step - 1], line_send.at[step], line_recv.at[step], peers[step]
        )

    def dispatch(step):
        if step:
            copies["plan", step].wait_recv()
            copies["line", step].wait_recv()
        block = line.at[step - 1] if step else tokens
        for p in far + (0,):
            slots = plans[step, pl.ds(experts[p], 1), :]
            pick = jnp.where(row_of == slots, 1.0, 0.0).astype(jnp.bfloat16)
            value = jnp.dot(pick, block[...], preferred_element_type=jnp.float32)
            value = value.astype(jnp.bfloat16)
            if p:
                picked[step, p - 1] = value
                copies["plane", step, p] = push(
                    picked.at[step, p - 1], rows.at[step, chunk(0, p)],
                    plane_send.at[step, p], plane_recv.at[step, p], plane[p],
                )
            else:
                rows[step, chunk(0, 0)] = value
                pass_on(step, 0)

    def pass_on(step, p):
        copies["core", step, p] = push(
            rows.at[step, chunk(0, p)], rows.at[step, chunk(1, p)],
            core_send.at[step, p], core_recv.at[step, p], partner,
        )

    def forward(step):
        for p in (1, 2, 3):
            copies["plane", step, p].wait_recv()
            pass_on(step, p)

    def compute(step):
        for p in range(4):
            copies["core", step, p].wait_recv()
        if step == 0:
            for copy in weights:
                copy.wait()
        block = rows.at[step]
        wide = 256

        def first(tile, carry):
            at = pl.ds(pl.multiple_of(tile * wide, wide), wide)
            gate = jnp.dot(block[...], gate_w[:, at], preferred_element_type=jnp.float32)
            up = jnp.dot(block[...], up_w[:, at], preferred_element_type=jnp.float32)
            hidden[:, at] = (gate / (1.0 + jnp.exp(-gate)) * up).astype(jnp.bfloat16)
            return carry

        lax.fori_loop(0, units // wide, first, 0)
        broad = 512

        def second(tile, carry):
            at = pl.ds(pl.multiple_of(tile * broad, broad), broad)
            value = jnp.dot(hidden[...], down_w[:, at], preferred_element_type=jnp.float32)
            result[step, :, at] = value.astype(jnp.bfloat16)
            return carry

        lax.fori_loop(0, width // broad, second, 0)
        copies["pair", step] = push(
            result.at[step, half(1)], other.at[step],
            pair_send.at[step], pair_recv.at[step], partner,
        )

    def finish(step):
        copies["pair", step].wait_recv()
        for p in far + (0,):
            at = pl.ds(p * cap, cap)
            both = result[step, at].astype(jnp.float32) + other[step, at].astype(jnp.float32)
            if p:
                result[step, at] = both.astype(jnp.bfloat16)
                copies["back", step, p] = push(
                    result.at[step, at], back.at[step, at],
                    back_send.at[step, p], back_recv.at[step, p], plane[p],
                )
            else:
                back[step, at] = both.astype(jnp.bfloat16)

    def expand(step):
        spread = []
        for p in range(4):
            if p:
                copies["back", step, p].wait_recv()
            slots = plans[step, pl.ds(experts[p], 1), :]
            factors = plans[step, pl.ds(experts[p] + 4 * nz, 1), :]
            spread.append(jnp.where(row_of == slots, factors, 0.0))
        spread = jnp.concatenate(spread, axis=0).T
        high = spread.astype(jnp.bfloat16)
        low = (spread - high.astype(jnp.float32)).astype(jnp.bfloat16)
        total = jnp.dot(high, back[step], preferred_element_type=jnp.float32)
        total += jnp.dot(low, back[step], preferred_element_type=jnp.float32)
        if step:
            partial[0, step - 1] = total.astype(jnp.bfloat16)
            copies["home", step] = push(
                partial.at[0, step - 1], partial.at[1, step - 1],
                home_send.at[step], home_recv.at[step], peers[step],
            )
        return total

    weights = [
        pltpu.make_async_copy(source, target, weight_sem.at[i])
        for i, (source, target) in enumerate(((w_gate, gate_w), (w_up, up_w), (w_down, down_w)))
    ]
    greet(plane[1:] + [partner] + peers[1:])
    order = [nz // 2] + [step for step in range(1, nz) if step != nz // 2]
    for step in order[:-1]:
        spread_line(step)
    for copy in weights:
        copy.start()
    plans[0] = plan[...]
    dispatch(0)
    forward(0)
    spread_line(order[-1])
    compute(0)
    for step in order[:-1]:
        dispatch(step)
    for turn, step in enumerate(order):
        forward(step)
        if turn == 1:
            dispatch(order[-1])
        if turn:
            finish(order[turn - 1])
        if turn > 1:
            expand(order[turn - 2])
        compute(step)
    finish(order[-1])
    finish(0)
    expand(order[-2])
    expand(order[-1])
    total = expand(0)
    for step in range(1, nz):
        copies["home", step].wait_recv()
        total += partial[1, step - 1].astype(jnp.float32)
    out[...] = total.astype(out.dtype)
    for copy in copies.values():
        copy.wait_send()


def expert_lines(tokens, routes, route_weights, w_gate, w_up, w_down):
    tok, width = tokens.shape
    topk = routes.shape[1]
    halves = lax.axis_size("ep")
    experts = halves // 2
    nz = halves // 8
    cap = tok * topk * 4 // (3 * experts)
    units = w_gate.shape[2]
    match = routes[None, :, :] == jnp.arange(experts, dtype=jnp.int32)[:, None, None]
    routed = jnp.any(match, axis=2)
    factor = jnp.sum(jnp.where(match, route_weights[None, :, :], 0.0), axis=2)
    earlier = jnp.triu(jnp.ones((tok, tok), jnp.bfloat16), 1)
    slot = jnp.dot(routed.astype(jnp.bfloat16), earlier, preferred_element_type=jnp.float32)
    plan = jnp.concatenate([jnp.where(routed, slot, -1.0), factor], axis=0)
    vmem, anywhere = pl.BlockSpec(memory_space=pltpu.VMEM), pl.BlockSpec(memory_space=pl.ANY)
    dma = pltpu.SemaphoreType.DMA
    half_type = jnp.bfloat16
    return pl.pallas_call(
        functools.partial(experts_kernel, nz, cap),
        out_shape=jax.ShapeDtypeStruct((tok, width), half_type),
        in_specs=[vmem, vmem, anywhere, anywhere, anywhere],
        out_specs=vmem,
        scratch_shapes=[
            pltpu.VMEM((nz, 2 * experts, tok), jnp.float32),
            pltpu.VMEM((nz - 1, tok, width), half_type),
            pltpu.VMEM((nz, 3, cap, width), half_type),
            pltpu.VMEM((nz, 8 * cap, width), half_type),
            pltpu.VMEM((8 * cap, units), half_type),
            pltpu.VMEM((nz, 8 * cap, width), half_type),
            pltpu.VMEM((nz, 4 * cap, width), half_type),
            pltpu.VMEM((nz, 4 * cap, width), half_type),
            pltpu.VMEM((2, nz - 1, tok, width), half_type),
            pltpu.VMEM((width, units), half_type),
            pltpu.VMEM((width, units), half_type),
            pltpu.VMEM((units, width), half_type),
            dma((3,)), dma((nz,)), dma((nz,)), dma((nz,)), dma((nz,)),
            dma((nz, 4)), dma((nz, 4)), dma((nz, 4)), dma((nz, 4)),
            dma((nz,)), dma((nz,)), dma((nz, 4)), dma((nz, 4)), dma((nz,)), dma((nz,)),
        ],
        compiler_params=pltpu.CompilerParams(
            collective_id=0, has_side_effects=True, vmem_limit_bytes=63 << 20
        ),
    )(tokens, plan, w_gate[0], w_up[0], w_down[0])


def shards(
    tokens, routes, route_weights, w_gate, w_up, w_down, queries, key_cache, value_cache, lengths
):
    if lax.axis_size("kv") == 1:
        moe_out = expert_lines(tokens, routes, route_weights, w_gate, w_up, w_down)
        return (moe_out, attend(queries, key_cache, value_cache, lengths))
    tok = tokens.shape[0]
    width = tokens.shape[1]
    topk = routes.shape[1]
    halves = lax.axis_size("ep")
    shares = lax.axis_size("kv")
    experts = halves // 2
    cap = tok * topk * 4 // (3 * experts)
    share_cap = cap // shares
    kv_index = lax.axis_index("kv")
    chosen = routes.reshape(-1)
    onehot = (chosen[:, None] == jnp.arange(experts, dtype=jnp.int32)[None, :]).astype(jnp.int32)
    before = jnp.cumsum(onehot, axis=0) - onehot
    slot = jnp.sum(before * onehot, axis=1)
    owner = jnp.arange(tok * topk, dtype=jnp.int32) // topk
    pick = jnp.full((experts * cap,), tok, jnp.int32).at[chosen * cap + slot].set(owner)
    padded = jnp.concatenate([tokens, jnp.zeros((1, width), tokens.dtype)], axis=0)
    outgoing = padded[pick].reshape(experts, cap, width)
    arrived = lax.all_to_all(
        jnp.repeat(outgoing, 2, axis=0), "ep", split_axis=0, concat_axis=0, tiled=True
    )
    flat_rows = arrived.reshape(halves * cap, width)
    partial_out = expert_math(flat_rows, w_gate[0], w_up[0], w_down[0]).reshape(halves, cap, width)
    half_out = lax.psum_scatter(
        partial_out.astype(jnp.bfloat16), "kv", scatter_dimension=1, tiled=True
    )
    back = lax.all_to_all(half_out, "ep", split_axis=0, concat_axis=0, tiled=True)
    table = back.reshape(halves * share_cap, width)
    local_slot = slot - kv_index * share_cap
    held = (local_slot >= 0) & (local_slot < share_cap)
    safe_slot = jnp.where(held, local_slot, 0)
    first_row = 2 * chosen * share_cap + safe_slot
    both = table[first_row].astype(jnp.float32) + table[first_row + share_cap].astype(jnp.float32)
    factor = jnp.where(held, route_weights.reshape(-1), 0.0)
    weighted = both * factor[:, None]
    summed = jnp.sum(weighted.reshape(tok, topk, width), axis=1)
    moe_out = lax.psum(summed.astype(jnp.bfloat16), "kv")
    attn_out = attend(queries, key_cache, value_cache, lengths)
    return (moe_out, attn_out)


def solution(mesh):
    return jax.shard_map(
        shards,
        mesh=mesh,
        in_specs=(
            P("ep", None),
            P("ep", None),
            P("ep", None),
            P("ep", None, "kv"),
            P("ep", None, "kv"),
            P("ep", "kv", None),
            P("ep", None),
            P("ep", "kv", None),
            P("ep", "kv", None),
            P("ep"),
        ),
        out_specs=(P("ep", None), P("ep", None)),
        check_vma=False,
    )
```
